256 devices in a mesh: ctx: 64 (over y, z, core), kv: 4 (over x).
Axes of the slice: x: 4, y: 4, z: 8, core: 2. Of those that a mesh axis runs over, the one named last changes fastest.
Arguments:
- queries: bfloat16 [32768, 4, 2048], P('ctx', 'kv'), may hold values from -480 to 480
- keys: bfloat16 [32768, 4, 128], P('ctx', 'kv'), may hold values from -6 to 6
- values: bfloat16 [32768, 4, 128], P('ctx', 'kv'), may hold values from -6 to 6
- inputs: bfloat16 [32768, 4608], P('ctx', 'kv'), may hold values from -6 to 6
- gate_weight: bfloat16 [4608, 4, 32], P('kv'), may hold values from -0.09375 to 0.09375
- comp_one: bfloat16 [4, 2, 4096, 256], P('kv'), may hold values from -0.09375 to 0.09375
- comp_two: bfloat16 [4, 2, 256, 128], P('kv'), may hold values from -0.375 to 0.375
Outputs:
- attended: bfloat16 [32768, 4, 2048], P('ctx', 'kv')
The draws below stay inside these ranges and needn't reach their ends.
All inputs are finite; a program needn't handle non-finite values.
Results may differ from the reference program's by a relative error of at most 0.0074.
Values may be sent and summed in bfloat16 or wider, within the bound.
A program may use at most 256 MiB of HBM per device.

```python
import math
import jax
import jax.numpy as jnp
from jax import lax

D = 4608
HEADS_G = 16
HD = 128
HID = 256
BLOCK = 32
STRIDE = 16
WINDOW = 512
GROUPS = 4
TOKENS = 32768


def draw_queries(key, part):
    base = jnp.clip(jax.random.normal(key, (TOKENS, GROUPS, HEADS_G * HD), jnp.float32), -6.0, 6.0)
    return base.astype(jnp.bfloat16)


def shard_levels(rng, extent, shards, smallest, high):
    gain, own = 1.0, jax.random.fold_in(rng, 6)
    for position, shards_of in shards:
        draws = jnp.exp(jax.random.uniform(jax.random.fold_in(own, position), (shards_of,), jnp.float32, smallest / len(shards), high / len(shards)))
        gain = gain * jnp.repeat(draws, extent[position] // shards_of).reshape([-1 if axis == position else 1 for axis in range(len(extent))])
    return gain


def noise(key, extent, spread, reach, cuts=(), kind=jnp.bfloat16):
    loudness = shard_levels(key, extent, cuts, -0.22, 0.18) if cuts else 1.0
    entries = jax.random.normal(key, extent, jnp.float32) * spread * loudness
    return jnp.minimum(jnp.maximum(entries, -reach), reach).astype(kind)


def setup_inputs(seed: int = 0) -> dict:
    splits = jax.random.split(jax.random.key(seed), 8)
    queries = draw_queries(jax.random.fold_in(splits[7], 71), 0)
    keys = noise(splits[1], (TOKENS, GROUPS, HD), 1.0, 6.0, ((0, 64), (1, 4)))
    values = noise(splits[2], (TOKENS, GROUPS, HD), 1.0, 6.0, ((0, 64), (1, 4)))
    inputs = noise(splits[3], (TOKENS, D), 1.0, 6.0, ((0, 64), (1, 4)))
    gate_weight = noise(splits[4], (D, GROUPS, 2 * HEADS_G), D ** -0.5, 0.09375, ((0, 4),))
    comp_one = noise(splits[5], (GROUPS, 2, BLOCK * HD, HID), (BLOCK * HD) ** -0.5, 0.09375, ((0, 4),))
    comp_two = noise(splits[6], (GROUPS, 2, HID, HD), HID ** -0.5, 0.375, ((0, 4),))
    return dict(queries=queries, keys=keys, values=values, inputs=inputs, gate_weight=gate_weight, comp_one=comp_one, comp_two=comp_two)


def compress(tokens_in, w_one, w_two):
    count = tokens_in.shape[0] // STRIDE
    split_rows = tokens_in.reshape(count, STRIDE, tokens_in.shape[1])
    blocks = jnp.concatenate([split_rows[:-1], split_rows[1:]], axis=1)
    flat = blocks.reshape(count - 1, BLOCK * tokens_in.shape[1])
    hidden = jax.nn.gelu(jnp.dot(flat, w_one, preferred_element_type=jnp.float32)).astype(jnp.bfloat16)
    return jnp.dot(hidden, w_two, preferred_element_type=jnp.float32).astype(jnp.bfloat16)


def rounded(array):
    return lax.optimization_barrier(array.astype(jnp.bfloat16)).astype(jnp.float32)


def one_group(operands):
    q_group, k_group, v_group, w_one, w_two, logits = operands
    length = q_group.shape[0]
    scale = HD ** -0.5
    comp_keys = compress(k_group, w_one[0], w_two[0]).astype(jnp.float32)
    comp_values = compress(v_group, w_one[1], w_two[1]).astype(jnp.float32)
    block_last = jnp.arange(comp_keys.shape[0], dtype=jnp.int32) * STRIDE + BLOCK - 1
    key_pad = jnp.concatenate([jnp.zeros((WINDOW, HD), jnp.bfloat16), k_group]).astype(jnp.float32)
    value_pad = jnp.concatenate([jnp.zeros((WINDOW, HD), jnp.bfloat16), v_group]).astype(jnp.float32)
    span = math.gcd(length, 512)

    def one_block(number):
        offset = number * span
        query = lax.dynamic_slice_in_dim(q_group, offset, span, 0).astype(jnp.float32).reshape(span, HEADS_G, HD)
        token_pos = offset + jnp.arange(span, dtype=jnp.int32)
        key_part = lax.dynamic_slice_in_dim(key_pad, offset, WINDOW + span, 0)
        value_part = lax.dynamic_slice_in_dim(value_pad, offset, WINDOW + span, 0)
        key_pos = offset - WINDOW + jnp.arange(WINDOW + span, dtype=jnp.int32)
        visible = (key_pos[None, :] > token_pos[:, None] - WINDOW) & (key_pos[None, :] <= token_pos[:, None]) & (key_pos[None, :] >= 0)
        scores = jnp.einsum('rhd,cd->rhc', query, key_part) * scale
        scores = jnp.where(visible[:, None, :], scores, -jnp.inf)
        top = jnp.max(scores, axis=-1, keepdims=True)
        expos = jnp.exp(scores - top)
        total = jnp.sum(expos, axis=-1, keepdims=True)
        near = jnp.einsum('rhc,cd->rhd', rounded(expos), value_part) / total
        far_scores = jnp.einsum('rhd,jd->rhj', query, comp_keys) * scale
        seen = block_last[None, :] <= token_pos[:, None]
        far_scores = jnp.where(seen[:, None, :], far_scores, -jnp.inf)
        far_top = jnp.maximum(jnp.max(far_scores, axis=-1, keepdims=True), 0.0)
        far_expos = jnp.exp(far_scores - far_top)
        far_total = jnp.exp(-far_top) + jnp.sum(far_expos, axis=-1, keepdims=True)
        far = jnp.einsum('rhj,jd->rhd', rounded(far_expos), comp_values) / far_total
        gates = jax.nn.sigmoid(lax.dynamic_slice_in_dim(logits, offset, span, 0))
        mixed = gates[:, :HEADS_G, None] * far + gates[:, HEADS_G:, None] * near
        return mixed.reshape(span, HEADS_G * HD).astype(jnp.bfloat16)

    result = lax.map(one_block, jnp.arange(length // span, dtype=jnp.int32))
    return result.reshape(length, HEADS_G * HD)


def reference(queries, keys, values, inputs, gate_weight, comp_one, comp_two):
    logits = jnp.dot(inputs, gate_weight.reshape(gate_weight.shape[0], -1), preferred_element_type=jnp.float32)
    logits = logits.reshape(inputs.shape[0], GROUPS, 2 * HEADS_G)
    operands = (queries.transpose(1, 0, 2), keys.transpose(1, 0, 2), values.transpose(1, 0, 2), comp_one, comp_two, logits.transpose(1, 0, 2))
    result = lax.map(one_group, operands)
    return result.transpose(1, 0, 2)
```

```python
import functools

import jax
import jax.numpy as jnp
from jax import lax
from jax.experimental import pallas as pl
from jax.experimental.pallas import tpu as pltpu
from jax.sharding import PartitionSpec as P

MESH = pl.DeviceIdType.MESH
F32 = jnp.float32
BF16 = jnp.bfloat16
BLOCK = 32
STRIDE = 16
WINDOW = 512
NEG = -1e30
LOG2E = 1.4426950408889634
NT = (((1,), (1,)), ((), ()))
KC = 512
HALF = 256


def kernel(
    dims,
    q_hbm, keys_hbm, values_hbm, inputs_hbm, gate_w_hbm, one_hbm, two_hbm,
    out_hbm,
    q_v, out_v, inp_v, gw_v, one_v, two_v,
    wk, wv, rim, kv_f32, wvt, gath, cvt, gate_send, gate_recv, gates,
    s0, s1, c0, c1, m_ref, acc_ref, near_ref, far_bias, near_bias,
    in_sem, out_sem, rim_sem, win_sem, gate_sem, y1_sem, z1_sem, z2_sem, y2_sem, core_sem,
):
    ny, nz, nc, nkv, heads = dims
    n_ctx = ny * nz * nc
    me = lax.axis_index("ctx")
    group = lax.axis_index("kv")
    y, z, core = me // (nz * nc), (me // nc) % nz, me % nc
    tok = q_v.shape[0]
    hd = wk.shape[1]
    scale = hd ** -0.5 * LOG2E
    right, left = lax.rem(me + 1, n_ctx), lax.rem(me + n_ctx - 1, n_ctx)

    def ctx_of(yy, zz, cc):
        return (yy * nz + zz) * nc + cc

    y_peer = lambda d: ctx_of(lax.rem(y + d, ny), z, core)
    z_peer = lambda d: ctx_of(y, lax.rem(z + d, nz), core)
    partner = ctx_of(y, z, 1 - core)
    kv_peer = lambda d: lax.rem(group + d, nkv)

    def load(src, dst, n):
        return pltpu.make_async_copy(src, dst, in_sem.at[n])

    loads = [
        load(keys_hbm, wk.at[pl.ds(WINDOW, tok), :], 0),
        load(values_hbm, wv.at[pl.ds(WINDOW, tok), :], 1),
        load(inputs_hbm, inp_v, 2),
        load(gate_w_hbm, gw_v, 3),
        load(one_hbm.at[0], one_v.at[0], 4),
        load(one_hbm.at[1], one_v.at[1], 5),
        load(two_hbm, two_v, 6),
        load(q_hbm, q_v, 7),
    ]
    for c in loads:
        c.start()

    barrier = pltpu.get_barrier_semaphore()
    n_sig = 0
    for d in range(1, ny):
        pl.semaphore_signal(barrier, inc=1, device_id={"ctx": y_peer(d)}, device_id_type=MESH)
        n_sig += 1
    for d in range(1, nz):
        pl.semaphore_signal(barrier, inc=1, device_id={"ctx": z_peer(d)}, device_id_type=MESH)
        n_sig += 1
    for other in (partner, left, right):
        pl.semaphore_signal(barrier, inc=1, device_id={"ctx": other}, device_id_type=MESH)
        n_sig += 1
    for d in range(1, nkv):
        pl.semaphore_signal(barrier, inc=1, device_id={"kv": kv_peer(d)}, device_id_type=MESH)
        n_sig += 1

    loads[2].wait()
    loads[3].wait()
    part = lax.dot_general(gw_v[...], inp_v[...], NT, preferred_element_type=F32)
    gate_send[...] = part.astype(BF16).reshape(gate_send.shape)
    loads[0].wait()
    loads[1].wait()

    pl.semaphore_wait(barrier, n_sig)

    def remote(src, dst, sems, n, **where):
        return pltpu.make_async_remote_copy(
            src_ref=src, dst_ref=dst, send_sem=sems.at[0, n], recv_sem=sems.at[1, n],
            device_id=where, device_id_type=MESH,
        )

    tail = pl.ds(WINDOW + tok - STRIDE, STRIDE)
    rim_k = remote(wk.at[tail, :], rim.at[0], rim_sem, 0, ctx=right)
    rim_v = remote(wv.at[tail, :], rim.at[1], rim_sem, 1, ctx=right)
    rim_k.start()
    rim_v.start()
    gate_copies = []
    for d in range(1, nkv):
        to = kv_peer(d)
        gate_copies.append(remote(gate_send.at[to], gate_recv.at[d], gate_sem, d, kv=to))
        gate_copies[-1].start()
    win_k = remote(wk.at[pl.ds(tok, WINDOW), :], wk.at[pl.ds(0, WINDOW), :], win_sem, 0, ctx=right)
    win_v = remote(wv.at[pl.ds(tok, WINDOW), :], wv.at[pl.ds(0, WINDOW), :], win_sem, 1, ctx=right)
    win_k.start()
    win_v.start()

    kv_f32[0, pl.ds(STRIDE, tok), :] = wk[pl.ds(WINDOW, tok), :].astype(F32)
    kv_f32[1, pl.ds(STRIDE, tok), :] = wv[pl.ds(WINDOW, tok), :].astype(F32)
    rim_k.wait()
    rim_v.wait()
    kv_f32[0, :STRIDE, :] = rim[0].astype(F32)
    kv_f32[1, :STRIDE, :] = rim[1].astype(F32)
    loads[6].wait()
    nb = tok // STRIDE
    row = lax.broadcasted_iota(jnp.int32, (nb, hd), 0)
    for s in range(2):
        flat = jnp.concatenate(
            [kv_f32[s, pl.ds(b, nb, stride=STRIDE), :] for b in range(BLOCK)], axis=1
        ).astype(BF16)
        loads[4 + s].wait()
        hidden = jnp.dot(flat, one_v[s], preferred_element_type=F32)
        hidden = jax.nn.gelu(hidden).astype(BF16)
        packed = jnp.dot(hidden, two_v[s], preferred_element_type=F32)
        packed = jnp.where((row == 0) & (me == 0), 0.0, packed)
        gath[s, y, z, core] = packed.astype(BF16)

    k1 = [remote(gath.at[0, y, z, core], gath.at[0, y, z, core], y1_sem, d, ctx=y_peer(d)) for d in range(1, ny)]
    v1 = [remote(gath.at[1, y, z, core], gath.at[1, y, z, core], z1_sem, d, ctx=z_peer(d)) for d in range(1, nz)]
    for c in k1 + v1:
        c.start()

    nfull = (me * nb) // KC
    ids = lax.broadcasted_iota(jnp.int32, (KC, tok), 0) + nfull * KC
    at = lax.broadcasted_iota(jnp.int32, (KC, tok), 1) + tok * me
    far_bias[...] = jnp.where((ids * STRIDE + STRIDE - 1 <= at) | (ids == 0), 0.0, NEG)
    width = WINDOW + HALF
    for i in range(tok // HALF):
        w = lax.broadcasted_iota(jnp.int32, (width, HALF), 0)
        t = lax.broadcasted_iota(jnp.int32, (width, HALF), 1)
        low = jnp.where(me == 0, WINDOW - i * HALF, 0)
        near_bias[:, i * HALF : (i + 1) * HALF] = jnp.where(
            (w > t) & (w <= t + WINDOW) & (w >= low), 0.0, NEG
        )
    extra = wvt.shape[0] - hd
    one_row = lambda n: jnp.where(
        lax.broadcasted_iota(jnp.int32, (extra, n), 0) == 0, 1.0, 0.0
    ).astype(BF16)
    wvt[hd:, :] = one_row(WINDOW + tok)
    cvt[hd:, :] = one_row(cvt.shape[1])
    wvt[:hd, WINDOW:] = kv_f32[1, pl.ds(STRIDE, tok), :].T.astype(BF16)

    logits = gate_send[group].astype(F32)
    for d in range(1, nkv):
        gate_copies[d - 1].wait()
        logits = logits + gate_recv[d].astype(F32)
    gates[...] = jax.nn.sigmoid(logits)

    win_k.wait()
    win_v.wait()
    wvt[:hd, :WINDOW] = wv[:WINDOW, :].astype(F32).T.astype(BF16)
    loads[7].wait()

    k2 = [remote(gath.at[0, :, z, core], gath.at[0, :, z, core], z2_sem, d, ctx=z_peer(d)) for d in range(1, nz)]
    v2 = [remote(gath.at[1, y, :, core], gath.at[1, y, :, core], y2_sem, d, ctx=y_peer(d)) for d in range(1, ny)]
    swap = remote(gath.at[:, :, :, core], gath.at[:, :, :, core], core_sem, 0, ctx=partner)

    def second():
        for c in k1 + v1:
            c.wait()
        for c in k2 + v2:
            c.start()

    def third():
        for c in k2 + v2:
            c.wait()
        swap.start()

    def head_cols(h):
        return pl.ds(pl.multiple_of(h * hd, hd), hd)

    def fold(s):
        return jnp.max(s.reshape(s.shape[0] // 8, 8, s.shape[1]), axis=0)

    def near_scores(h, s_ref, c_ref):
        for i in range(tok // HALF):
            cols = slice(i * HALF, (i + 1) * HALF)
            s = lax.dot_general(
                wk[i * HALF : i * HALF + width, :], q_v[cols, head_cols(h)], NT,
                preferred_element_type=F32,
            )
            s = s + near_bias[:, cols]
            s_ref[:, cols] = s
            c_ref[:, cols] = fold(s)

    def near_values(h, s_ref, c_ref):
        m = jnp.max(c_ref[...], axis=0, keepdims=True) * scale
        e = jnp.exp2(s_ref[...] * scale - m).astype(BF16)
        for i in range(tok // HALF):
            cols = slice(i * HALF, (i + 1) * HALF)
            o = jnp.dot(wvt[:, i * HALF : i * HALF + width], e[:, cols], preferred_element_type=F32)
            near_ref[h, :, cols] = o[:hd] * (gates[pl.ds(heads + h, 1), cols] / o[hd : hd + 1])

    near_scores(0, s0, c0)

    def near_pair(j, carry):
        h = 2 * j
        near_scores(h + 1, s1, c1)
        near_values(h, s0, c0)
        near_scores(jnp.minimum(h + 2, heads - 2), s0, c0)
        near_values(h + 1, s1, c1)
        pl.when(j == STEP2)(second)
        pl.when(j == STEP3)(third)
        return carry

    lax.fori_loop(0, heads // 2, near_pair, 0)

    swap.wait()
    per_y = nz * nc * nb
    for i in range(ny):
        vals = gath[1, i].reshape(per_y, hd)
        cvt[:hd, i * per_y : (i + 1) * per_y] = vals.astype(F32).T.astype(BF16)

    m_ref[...] = jnp.zeros_like(m_ref)
    acc_ref[...] = jnp.zeros_like(acc_ref)

    def far_scores(c, h, s_ref, c_ref, masked):
        k = gath[0, c].reshape(KC, hd)
        s = lax.dot_general(k, q_v[:, head_cols(h)], NT, preferred_element_type=F32)
        if masked:
            s = s + far_bias[...]
        s_ref[:KC, :] = s
        c_ref[...] = fold(s)

    def far_values(c, h, s_ref, c_ref):
        m_old = m_ref[pl.ds(h, 1), :]
        m = jnp.maximum(jnp.max(c_ref[...], axis=0, keepdims=True) * scale, m_old)
        e = jnp.exp2(s_ref[:KC, :] * scale - m).astype(BF16)
        vt = cvt[:, pl.ds(pl.multiple_of(c * KC, KC), KC)]
        o = jnp.dot(vt, e, preferred_element_type=F32)
        acc_ref[h] = acc_ref[h] * jnp.exp2(m_old - m) + o
        m_ref[pl.ds(h, 1), :] = m

    def far_sweep(chunk_of, head_of, count, masked):
        far_scores(chunk_of(0), head_of(0), s0, c0, masked)

        def pair(j, carry):
            n = 2 * j
            far_scores(chunk_of(n + 1), head_of(n + 1), s1, c1, masked)
            far_values(chunk_of(n), head_of(n), s0, c0)
            nxt = jnp.minimum(n + 2, count - 2)
            far_scores(chunk_of(nxt), head_of(nxt), s0, c0, masked)
            far_values(chunk_of(n + 1), head_of(n + 1), s1, c1)
            return carry

        lax.fori_loop(0, count // 2, pair, 0)

    @pl.when(nfull > 0)
    def _():
        far_sweep(lambda n: n // heads, lambda n: lax.rem(n, heads), nfull * heads, False)

    far_sweep(lambda n: nfull, lambda n: n, heads, True)

    def put(h):
        return pltpu.make_async_copy(out_v.at[:, head_cols(h)], out_hbm.at[:, head_cols(h)], out_sem.at[h])

    def finish(h, carry):
        o = acc_ref[h]
        r = o[:hd] * (gates[pl.ds(h, 1), :] / o[hd : hd + 1]) + near_ref[h]
        out_v[:, head_cols(h)] = r.T.astype(BF16)
        put(h).start()
        return carry

    lax.fori_loop(0, heads, finish, 0)
    for h in range(heads):
        put(h).wait()


STEP2, STEP3 = 2, 6


def on_device(dims, queries, keys, values, inputs, gate_weight, comp_one, comp_two):
    ny, nz, nc, nkv, heads = dims
    tok = queries.shape[0]
    hd = keys.shape[2]
    depth = inputs.shape[1]
    hid = comp_one.shape[3]
    gate_rows = gate_weight.shape[1] * gate_weight.shape[2]
    cols = ny * nz * nc * (tok // STRIDE)
    q = queries.reshape(tok, heads * hd)
    gate_w = gate_weight.transpose(1, 2, 0).reshape(gate_rows, depth)
    any_spec = pl.BlockSpec(memory_space=pl.ANY)
    vm = pltpu.VMEM
    dma = pltpu.SemaphoreType.DMA
    width = WINDOW + HALF
    out = pl.pallas_call(
        functools.partial(kernel, dims),
        out_shape=jax.ShapeDtypeStruct((tok, heads * hd), BF16),
        in_specs=[any_spec] * 7,
        out_specs=any_spec,
        scratch_shapes=[
            vm((tok, heads * hd), BF16),
            vm((tok, heads * hd), BF16),
            vm((tok, depth), BF16),
            vm((gate_rows, depth), BF16),
            vm((2, BLOCK * hd, hid), BF16),
            vm((2, hid, hd), BF16),
            vm((WINDOW + tok, hd), BF16),
            vm((WINDOW + tok, hd), BF16),
            vm((2, STRIDE, hd), BF16),
            vm((2, STRIDE + tok, hd), F32),
            vm((hd + 16, WINDOW + tok), BF16),
            vm((2, ny, nz, nc, tok // STRIDE, hd), BF16),
            vm((hd + 16, cols), BF16),
            vm((nkv, 2 * heads, tok), BF16),
            vm((nkv, 2 * heads, tok), BF16),
            vm((2 * heads, tok), F32),
            vm((width, tok), F32),
            vm((width, tok), F32),
            vm((8, tok), F32),
            vm((8, tok), F32),
            vm((heads, tok), F32),
            vm((heads, hd + 16, tok), F32),
            vm((heads, hd, tok), F32),
            vm((KC, tok), F32),
            vm((width, tok), F32),
            dma((8,)),
            dma((heads,)),
            dma((2, 2)),
            dma((2, 2)),
            dma((2, nkv)),
            dma((2, ny)),
            dma((2, nz)),
            dma((2, nz)),
            dma((2, ny)),
            dma((2, 1)),
        ],
        compiler_params=pltpu.CompilerParams(
            collective_id=0, has_side_effects=True, vmem_limit_bytes=58 * 1024 * 1024
        ),
        name="attend",
    )(
        q,
        keys.reshape(tok, hd),
        values.reshape(tok, hd),
        inputs,
        gate_w,
        comp_one.reshape(comp_one.shape[1:]),
        comp_two.reshape(comp_two.shape[1:]),
    )
    return out.reshape(tok, 1, heads * hd)


def solution(mesh):
    placed = (
        P("ctx", "kv", None),
        P("ctx", "kv", None),
        P("ctx", "kv", None),
        P("ctx", "kv"),
        P("kv", None, None),
        P("kv", None, None, None),
        P("kv", None, None, None),
    )
    dims = (4, mesh.shape["ctx"] // 8, 2, mesh.shape["kv"], 16)
    return jax.shard_map(
        functools.partial(on_device, dims),
        mesh=mesh, in_specs=placed, out_specs=P("ctx", "kv", None), check_vma=False,
    )
```

```python
import functools

import jax
import jax.numpy as jnp
from jax import lax
from jax.experimental import pallas as pl
from jax.experimental.pallas import tpu as pltpu
from jax.sharding import PartitionSpec as P

MESH = pl.DeviceIdType.MESH
F32 = jnp.float32
BF16 = jnp.bfloat16
BLOCK = 32
STRIDE = 16
WINDOW = 512
NEG = -1e30
LOG2E = 1.4426950408889634
NT = (((1,), (1,)), ((), ()))
KC = 512
HALF = 256


def kernel(
    dims,
    q_hbm, keys_hbm, values_hbm, inputs_hbm, gate_w_hbm, one_hbm, two_hbm,
    out_hbm,
    q_v, out_v, inp_v, gw_v, one_v, two_v,
    wk, wv, rim, kv_f32, wvt, gath, cvt, gate_send, gate_recv, gates,
    s0, s1, c0, c1, m_ref, acc_ref, near_ref, far_bias, near_bias,
    in_sem, out_sem, rim_sem, win_sem, gate_sem, y1_sem, z1_sem, z2_sem, y2_sem, core_sem,
):
    ny, nz, nc, nkv, heads = dims
    n_ctx = ny * nz * nc
    me = lax.axis_index("ctx")
    group = lax.axis_index("kv")
    y, z, core = me // (nz * nc), (me // nc) % nz, me % nc
    tok = q_v.shape[0]
    hd = wk.shape[1]
    scale = hd ** -0.5 * LOG2E
    right, left = lax.rem(me + 1, n_ctx), lax.rem(me + n_ctx - 1, n_ctx)

    def ctx_of(yy, zz, cc):
        return (yy * nz + zz) * nc + cc

    y_peer = lambda d: ctx_of(lax.rem(y + d, ny), z, core)
    z_peer = lambda d: ctx_of(y, lax.rem(z + d, nz), core)
    partner = ctx_of(y, z, 1 - core)
    kv_peer = lambda d: lax.rem(group + d, nkv)

    def load(src, dst, n):
        return pltpu.make_async_copy(src, dst, in_sem.at[n])

    loads = [
        load(keys_hbm, wk.at[pl.ds(WINDOW, tok), :], 0),
        load(values_hbm, wv.at[pl.ds(WINDOW, tok), :], 1),
        load(one_hbm.at[0], one_v.at[0], 2),
        load(one_hbm.at[1], one_v.at[1], 3),
        load(two_hbm, two_v, 4),
        load(q_hbm, q_v, 7),
        load(inputs_hbm, inp_v, 5),
        load(gate_w_hbm, gw_v, 6),
    ]
    for c in loads:
        c.start()

    barrier = pltpu.get_barrier_semaphore()
    n_sig = 0
    for d in range(1, ny):
        pl.semaphore_signal(barrier, inc=1, device_id={"ctx": y_peer(d)}, device_id_type=MESH)
        n_sig += 1
    for d in range(1, nz):
        pl.semaphore_signal(barrier, inc=1, device_id={"ctx": z_peer(d)}, device_id_type=MESH)
        n_sig += 1
    for other in (partner, left, right):
        pl.semaphore_signal(barrier, inc=1, device_id={"ctx": other}, device_id_type=MESH)
        n_sig += 1
    for d in range(1, nkv):
        pl.semaphore_signal(barrier, inc=1, device_id={"kv": kv_peer(d)}, device_id_type=MESH)
        n_sig += 1

    loads[0].wait()
    loads[1].wait()
    kv_f32[0, pl.ds(STRIDE, tok), :] = wk[pl.ds(WINDOW, tok), :].astype(F32)
    kv_f32[1, pl.ds(STRIDE, tok), :] = wv[pl.ds(WINDOW, tok), :].astype(F32)

    pl.semaphore_wait(barrier, n_sig)

    def remote(src, dst, sems, n, **where):
        return pltpu.make_async_remote_copy(
            src_ref=src, dst_ref=dst, send_sem=sems.at[0, n], recv_sem=sems.at[1, n],
            device_id=where, device_id_type=MESH,
        )

    tail = pl.ds(WINDOW + tok - STRIDE, STRIDE)
    rim_k = remote(wk.at[tail, :], rim.at[0], rim_sem, 0, ctx=right)
    rim_v = remote(wv.at[tail, :], rim.at[1], rim_sem, 1, ctx=right)
    rim_k.start()
    rim_v.start()
    win_k = remote(wk.at[pl.ds(tok, WINDOW), :], wk.at[pl.ds(0, WINDOW), :], win_sem, 0, ctx=right)
    win_v = remote(wv.at[pl.ds(tok, WINDOW), :], wv.at[pl.ds(0, WINDOW), :], win_sem, 1, ctx=right)
    win_k.start()
    win_v.start()

    rim_k.wait()
    rim_v.wait()
    kv_f32[0, :STRIDE, :] = rim[0].astype(F32)
    kv_f32[1, :STRIDE, :] = rim[1].astype(F32)
    loads[4].wait()
    nb = tok // STRIDE
    row = lax.broadcasted_iota(jnp.int32, (nb, hd), 0)
    loads[2].wait()
    loads[3].wait()

    def squeeze(s, carry):
        flat = jnp.concatenate(
            [kv_f32[s, pl.ds(b, nb, stride=STRIDE), :] for b in range(BLOCK)], axis=1
        ).astype(BF16)
        hidden = jnp.dot(flat, one_v[s], preferred_element_type=F32)
        hidden = jax.nn.gelu(hidden).astype(BF16)
        packed = jnp.dot(hidden, two_v[s], preferred_element_type=F32)
        packed = jnp.where((row == 0) & (me == 0), 0.0, packed)
        gath[s, core, y, z] = packed.astype(BF16)
        return carry

    lax.fori_loop(0, 2, squeeze, 0)
    k1 = [remote(gath.at[0, core, y, z], gath.at[0, core, y, z], y1_sem, d, ctx=y_peer(d)) for d in range(1, ny)]
    v1 = [remote(gath.at[1, core, y, z], gath.at[1, core, y, z], z1_sem, d, ctx=z_peer(d)) for d in range(1, nz)]
    for c in k1 + v1:
        c.start()

    slot = y * nz + z
    per = KC // nb
    nfull = slot // per
    for par in range(nc):
        i = lax.broadcasted_iota(jnp.int32, (KC, tok), 0) + nfull * KC
        ids = (i // nb) * (nc * nb) + par * nb + lax.rem(i, nb)
        at = lax.broadcasted_iota(jnp.int32, (KC, tok), 1) + tok * me
        far_bias[par] = jnp.where((ids * STRIDE + STRIDE - 1 <= at) | (ids == 0), 0.0, NEG)
    width = WINDOW + HALF
    for i in range(tok // HALF):
        w = lax.broadcasted_iota(jnp.int32, (width, HALF), 0)
        t = lax.broadcasted_iota(jnp.int32, (width, HALF), 1)
        low = jnp.where(me == 0, WINDOW - i * HALF, 0)
        near_bias[:, i * HALF : (i + 1) * HALF] = jnp.where(
            (w > t) & (w <= t + WINDOW) & (w >= low), 0.0, NEG
        )
    extra = wvt.shape[0] - hd
    one_row = lambda n: jnp.where(
        lax.broadcasted_iota(jnp.int32, (extra, n), 0) == 0, 1.0, 0.0
    ).astype(BF16)
    wvt[hd:, :] = one_row(WINDOW + tok)
    cvt[hd:, :] = one_row(cvt.shape[1])
    wvt[:hd, WINDOW:] = kv_f32[1, pl.ds(STRIDE, tok), :].T.astype(BF16)

    loads[6].wait()
    loads[7].wait()
    part = lax.dot_general(gw_v[...], inp_v[...], NT, preferred_element_type=F32)
    gate_send[...] = part.astype(BF16).reshape(gate_send.shape)
    gate_copies = []
    for d in range(1, nkv):
        to = kv_peer(d)
        gate_copies.append(remote(gate_send.at[to], gate_recv.at[d], gate_sem, d, kv=to))
        gate_copies[-1].start()

    win_k.wait()
    win_v.wait()
    wvt[:hd, :WINDOW] = wv[:WINDOW, :].astype(F32).T.astype(BF16)
    loads[5].wait()

    k2 = [remote(gath.at[0, core, :, z], gath.at[0, core, :, z], z2_sem, d, ctx=z_peer(d)) for d in range(1, nz)]
    v2 = [remote(gath.at[1, core, y], gath.at[1, core, y], y2_sem, d, ctx=y_peer(d)) for d in range(1, ny)]
    swap = remote(gath.at[:, core], gath.at[:, core], core_sem, 0, ctx=partner)

    def second():
        for c in k1 + v1:
            c.wait()
        for c in k2 + v2:
            c.start()

    def third():
        for c in k2 + v2:
            c.wait()
        swap.start()

    def head_cols(h):
        return pl.ds(pl.multiple_of(h * hd, hd), hd)

    def fold(s):
        return jnp.max(s.reshape(s.shape[0] // 8, 8, s.shape[1]), axis=0)

    def near_scores(h, s_ref, c_ref):
        for i in range(tok // HALF):
            cols = slice(i * HALF, (i + 1) * HALF)
            s = lax.dot_general(
                wk[i * HALF : i * HALF + width, :], q_v[cols, head_cols(h)], NT,
                preferred_element_type=F32,
            )
            s = s + near_bias[:, cols]
            s_ref[:, cols] = s
            c_ref[:, cols] = fold(s)

    def near_values(h, s_ref, c_ref):
        m = jnp.max(c_ref[...], axis=0, keepdims=True) * scale
        e = jnp.exp2(s_ref[...] * scale - m).astype(BF16)
        for i in range(tok // HALF):
            cols = slice(i * HALF, (i + 1) * HALF)
            o = jnp.dot(wvt[:, i * HALF : i * HALF + width], e[:, cols], preferred_element_type=F32)
            near_ref[h, :, cols] = o[:hd] * (1.0 / o[hd : hd + 1])

    near_scores(0, s0, c0)

    def near_group(j, carry):
        for u in range(0, UNROLL, 2):
            h = UNROLL * j + u
            near_scores(h + 1, s1, c1)
            near_values(h, s0, c0)
            near_scores(jnp.minimum(h + 2, heads - 2), s0, c0)
            near_values(h + 1, s1, c1)
        pl.when(j == STEP2)(second)
        return carry

    lax.fori_loop(0, heads // UNROLL, near_group, 0)

    third()
    logits = gate_send[group].astype(F32)
    for d in range(1, nkv):
        gate_copies[d - 1].wait()
        logits = logits + gate_recv[d].astype(F32)
    gates[...] = jax.nn.sigmoid(logits)


    m_ref[...] = jnp.zeros_like(m_ref)
    acc_ref[...] = jnp.zeros_like(acc_ref)
    half = cvt.shape[1] // nc
    keys_all = gath.reshape(2, nc, half, hd)

    def far_scores(par, first, w, h, s_ref, c_ref, masked):
        k = keys_all[0, par, pl.ds(first, w), :]
        s = lax.dot_general(k, q_v[:, head_cols(h)], NT, preferred_element_type=F32)
        if masked:
            s = s + far_bias[par, :w, :]
        s_ref[:w, :] = s
        c_ref[...] = fold(s)

    def far_values(par, first, w, h, s_ref, c_ref, last):
        m_old = m_ref[pl.ds(h, 1), :]
        m = jnp.maximum(jnp.max(c_ref[...], axis=0, keepdims=True) * scale, m_old)
        e = jnp.exp2(s_ref[:w, :] * scale - m).astype(BF16)
        vt = cvt[:, pl.ds(pl.multiple_of(par * half + first, KC), w)]
        o = jnp.dot(vt, e, preferred_element_type=F32)
        o = acc_ref[h] * jnp.exp2(m_old - m) + o
        if last:
            r = o[:hd] * (gates[pl.ds(h, 1), :] / o[hd : hd + 1]) + near_ref[h] * gates[pl.ds(heads + h, 1), :]
            out_v[:, head_cols(h)] = r.T.astype(BF16)
        else:
            acc_ref[h] = o
            m_ref[pl.ds(h, 1), :] = m

    def put(h):
        return pltpu.make_async_copy(out_v.at[:, head_cols(h)], out_hbm.at[:, head_cols(h)], out_sem.at[h])

    def far_sweep(par, first, w, masked, last):
        far_scores(par, first, w, 0, s0, c0, masked)

        def group_of_heads(j, carry):
            for u in range(0, UNROLL, 2):
                h = UNROLL * j + u
                far_scores(par, first, w, h + 1, s1, c1, masked)
                far_values(par, first, w, h, s0, c0, last)
                far_scores(par, first, w, jnp.minimum(h + 2, heads - 2), s0, c0, masked)
                far_values(par, first, w, h + 1, s1, c1, last)
            if last:
                for u in range(UNROLL):
                    put(UNROLL * j + u).start()
            return carry

        lax.fori_loop(0, heads // UNROLL, group_of_heads, 0)

    for turn in range(nc):
        par = core if turn == 0 else 1 - core
        if turn:
            swap.wait()
        for i in range(ny):
            vals = gath[1, par, i].reshape(nz * nb, hd)
            cvt[:hd, pl.ds(pl.multiple_of(par * half + i * nz * nb, nz * nb), nz * nb)] = vals.astype(F32).T.astype(BF16)

        def whole(i, carry):
            far_sweep(par, pl.multiple_of(i * KC, KC), KC, False, False)
            return carry

        lax.fori_loop(0, nfull, whole, 0)
        rest = lax.rem(slot, per) * nb // PIECE
        for n in range(KC // PIECE):
            @pl.when(rest == n)
            def _():
                far_sweep(par, pl.multiple_of(nfull * KC, KC), (n + 1) * PIECE, True, turn == nc - 1)

    for h in range(heads):
        put(h).wait()


PIECE = 128
STEP2 = 0
UNROLL = 4


def on_device(dims, queries, keys, values, inputs, gate_weight, comp_one, comp_two):
    ny, nz, nc, nkv, heads = dims
    tok = queries.shape[0]
    hd = keys.shape[2]
    depth = inputs.shape[1]
    hid = comp_one.shape[3]
    gate_rows = gate_weight.shape[1] * gate_weight.shape[2]
    cols = ny * nz * nc * (tok // STRIDE)
    q = queries.reshape(tok, heads * hd)
    gate_w = gate_weight.transpose(1, 2, 0).reshape(gate_rows, depth)
    any_spec = pl.BlockSpec(memory_space=pl.ANY)
    vm = pltpu.VMEM
    dma = pltpu.SemaphoreType.DMA
    width = WINDOW + HALF
    out = pl.pallas_call(
        functools.partial(kernel, dims),
        out_shape=jax.ShapeDtypeStruct((tok, heads * hd), BF16),
        in_specs=[any_spec] * 7,
        out_specs=any_spec,
        scratch_shapes=[
            vm((tok, heads * hd), BF16),
            vm((tok, heads * hd), BF16),
            vm((tok, depth), BF16),
            vm((gate_rows, depth), BF16),
            vm((2, BLOCK * hd, hid), BF16),
            vm((2, hid, hd), BF16),
            vm((WINDOW + tok, hd), BF16),
            vm((WINDOW + tok, hd), BF16),
            vm((2, STRIDE, hd), BF16),
            vm((2, STRIDE + tok, hd), F32),
            vm((hd + 16, WINDOW + tok), BF16),
            vm((2, nc, ny, nz, tok // STRIDE, hd), BF16),
            vm((hd + 16, cols), BF16),
            vm((nkv, 2 * heads, tok), BF16),
            vm((nkv, 2 * heads, tok), BF16),
            vm((2 * heads, tok), F32),
            vm((width, tok), F32),
            vm((width, tok), F32),
            vm((8, tok), F32),
            vm((8, tok), F32),
            vm((heads, tok), F32),
            vm((heads, hd + 16, tok), F32),
            vm((heads, hd, tok), F32),
            vm((nc, KC, tok), F32),
            vm((width, tok), F32),
            dma((8,)),
            dma((heads,)),
            dma((2, 2)),
            dma((2, 2)),
            dma((2, nkv)),
            dma((2, ny)),
            dma((2, nz)),
            dma((2, nz)),
            dma((2, ny)),
            dma((2, 1)),
        ],
        compiler_params=pltpu.CompilerParams(
            collective_id=0, has_side_effects=True, vmem_limit_bytes=58 * 1024 * 1024
        ),
        name="attend",
    )(
        q,
        keys.reshape(tok, hd),
        values.reshape(tok, hd),
        inputs,
        gate_w,
        comp_one.reshape(comp_one.shape[1:]),
        comp_two.reshape(comp_two.shape[1:]),
    )
    return out.reshape(tok, 1, heads * hd)


def solution(mesh):
    placed = (
        P("ctx", "kv", None),
        P("ctx", "kv", None),
        P("ctx", "kv", None),
        P("ctx", "kv"),
        P("kv", None, None),
        P("kv", None, None, None),
        P("kv", None, None, None),
    )
    dims = (4, mesh.shape["ctx"] // 8, 2, mesh.shape["kv"], 16)
    return jax.shard_map(
        functools.partial(on_device, dims),
        mesh=mesh, in_specs=placed, out_specs=P("ctx", "kv", None), check_vma=False,
    )
```

```python
import functools

import jax
import jax.numpy as jnp
from jax import lax
from jax.experimental import pallas as pl
from jax.experimental.pallas import tpu as pltpu
from jax.sharding import PartitionSpec as P

MESH = pl.DeviceIdType.MESH
F32 = jnp.float32
BF16 = jnp.bfloat16
BLOCK = 32
STRIDE = 16
WINDOW = 512
NEG = -1e30
LOG2E = 1.4426950408889634
NT = (((1,), (1,)), ((), ()))
KC = 512
HALF = 256


def kernel(
    dims,
    q_hbm, keys_hbm, values_hbm, inputs_hbm, gate_w_hbm, one_hbm, two_hbm,
    out_v,
    q_v, inp_v, gw_v, one_v, two_v,
    wk, wv, rim, kv_f32, wvt, gath, cvt, gate_send, gate_recv, gates,
    s0, s1, c0, c1, m_ref, acc_ref, near_ref, far_bias, near_bias,
    in_sem, rim_sem, win_sem, gate_sem, y1_sem, z1_sem, z2_sem, y2_sem, core_sem,
):
    ny, nz, nc, nkv, heads = dims
    n_ctx = ny * nz * nc
    me = lax.axis_index("ctx")
    group = lax.axis_index("kv")
    y, z, core = me // (nz * nc), (me // nc) % nz, me % nc
    tok = q_v.shape[0]
    hd = wk.shape[1]
    scale = hd ** -0.5 * LOG2E
    right, left = lax.rem(me + 1, n_ctx), lax.rem(me + n_ctx - 1, n_ctx)

    def ctx_of(yy, zz, cc):
        return (yy * nz + zz) * nc + cc

    y_peer = lambda d: ctx_of(lax.rem(y + d, ny), z, core)
    z_peer = lambda d: ctx_of(y, lax.rem(z + d, nz), core)
    partner = ctx_of(y, z, 1 - core)
    kv_peer = lambda d: lax.rem(group + d, nkv)

    def load(src, dst, n):
        return pltpu.make_async_copy(src, dst, in_sem.at[n])

    loads = [
        load(keys_hbm, wk.at[pl.ds(WINDOW, tok), :], 0),
        load(values_hbm, wv.at[pl.ds(WINDOW, tok), :], 1),
        load(one_hbm.at[0], one_v.at[0], 2),
        load(one_hbm.at[1], one_v.at[1], 3),
        load(two_hbm, two_v, 4),
        load(q_hbm, q_v, 7),
        load(inputs_hbm, inp_v, 5),
        load(gate_w_hbm, gw_v, 6),
    ]
    for c in loads[:5]:
        c.start()

    barrier = pltpu.get_barrier_semaphore()
    n_sig = 0
    for d in range(1, ny):
        pl.semaphore_signal(barrier, inc=1, device_id={"ctx": y_peer(d)}, device_id_type=MESH)
        n_sig += 1
    for d in range(1, nz):
        pl.semaphore_signal(barrier, inc=1, device_id={"ctx": z_peer(d)}, device_id_type=MESH)
        n_sig += 1
    for other in (partner, left, right):
        pl.semaphore_signal(barrier, inc=1, device_id={"ctx": other}, device_id_type=MESH)
        n_sig += 1
    for d in range(1, nkv):
        pl.semaphore_signal(barrier, inc=1, device_id={"kv": kv_peer(d)}, device_id_type=MESH)
        n_sig += 1

    loads[0].wait()
    loads[1].wait()
    kv_f32[0, pl.ds(STRIDE, tok), :] = wk[pl.ds(WINDOW, tok), :].astype(F32)
    kv_f32[1, pl.ds(STRIDE, tok), :] = wv[pl.ds(WINDOW, tok), :].astype(F32)

    pl.semaphore_wait(barrier, n_sig)

    def remote(src, dst, sems, n, **where):
        return pltpu.make_async_remote_copy(
            src_ref=src, dst_ref=dst, send_sem=sems.at[0, n], recv_sem=sems.at[1, n],
            device_id=where, device_id_type=MESH,
        )

    tail = pl.ds(WINDOW + tok - STRIDE, STRIDE)
    rim_k = remote(wk.at[tail, :], rim.at[0], rim_sem, 0, ctx=right)
    rim_v = remote(wv.at[tail, :], rim.at[1], rim_sem, 1, ctx=right)
    rim_k.start()
    rim_v.start()
    win_k = remote(wk.at[pl.ds(tok, WINDOW), :], wk.at[pl.ds(0, WINDOW), :], win_sem, 0, ctx=right)
    win_v = remote(wv.at[pl.ds(tok, WINDOW), :], wv.at[pl.ds(0, WINDOW), :], win_sem, 1, ctx=right)
    win_k.start()
    win_v.start()

    rim_k.wait()
    rim_v.wait()
    kv_f32[0, :STRIDE, :] = rim[0].astype(F32)
    kv_f32[1, :STRIDE, :] = rim[1].astype(F32)
    loads[4].wait()
    nb = tok // STRIDE
    row = lax.broadcasted_iota(jnp.int32, (nb, hd), 0)
    loads[2].wait()
    loads[3].wait()
    for c in loads[5:]:
        c.start()

    def squeeze(s, carry):
        flat = jnp.concatenate(
            [kv_f32[s, pl.ds(b, nb, stride=STRIDE), :] for b in range(BLOCK)], axis=1
        ).astype(BF16)
        hidden = jnp.dot(flat, one_v[s], preferred_element_type=F32)
        hidden = jax.nn.gelu(hidden).astype(BF16)
        packed = jnp.dot(hidden, two_v[s], preferred_element_type=F32)
        packed = jnp.where((row == 0) & (me == 0), 0.0, packed)
        gath[s, core, y, z] = packed.astype(BF16)
        return carry

    lax.fori_loop(0, 2, squeeze, 0)
    k1 = [remote(gath.at[0, core, y, z], gath.at[0, core, y, z], y1_sem, d, ctx=y_peer(d)) for d in range(1, ny)]
    v1 = [remote(gath.at[1, core, y, z], gath.at[1, core, y, z], z1_sem, d, ctx=z_peer(d)) for d in range(1, nz)]
    for c in k1 + v1:
        c.start()

    slot = y * nz + z
    per = KC // nb
    nfull = slot // per
    for par in range(nc):
        i = lax.broadcasted_iota(jnp.int32, (KC, tok), 0) + nfull * KC
        ids = (i // nb) * (nc * nb) + par * nb + lax.rem(i, nb)
        at = lax.broadcasted_iota(jnp.int32, (KC, tok), 1) + tok * me
        far_bias[par] = jnp.where((ids * STRIDE + STRIDE - 1 <= at) | (ids == 0), 0.0, NEG)
    width = WINDOW + HALF
    for i in range(tok // HALF):
        w = lax.broadcasted_iota(jnp.int32, (width, HALF), 0)
        t = lax.broadcasted_iota(jnp.int32, (width, HALF), 1)
        low = jnp.where(me == 0, WINDOW - i * HALF, 0)
        near_bias[:, i * HALF : (i + 1) * HALF] = jnp.where(
            (w > t) & (w <= t + WINDOW) & (w >= low), 0.0, NEG
        )
    extra = wvt.shape[0] - hd
    one_row = lambda n: jnp.where(
        lax.broadcasted_iota(jnp.int32, (extra, n), 0) == 0, 1.0, 0.0
    ).astype(BF16)
    wvt[hd:, :] = one_row(WINDOW + tok)
    cvt[hd:, :] = one_row(cvt.shape[1])
    wvt[:hd, WINDOW:] = kv_f32[1, pl.ds(STRIDE, tok), :].T.astype(BF16)

    m_ref[...] = jnp.zeros_like(m_ref)

    def init(h, carry):
        acc_ref[h] = jnp.zeros(acc_ref.shape[1:], F32)
        return carry

    lax.fori_loop(0, heads, init, 0)
    loads[6].wait()
    loads[7].wait()
    part = lax.dot_general(gw_v[...], inp_v[...], NT, preferred_element_type=F32)
    gate_send[...] = part.astype(BF16).reshape(gate_send.shape)
    gate_copies = []
    for d in range(1, nkv):
        to = kv_peer(d)
        gate_copies.append(remote(gate_send.at[to], gate_recv.at[d], gate_sem, d, kv=to))
        gate_copies[-1].start()

    win_k.wait()
    win_v.wait()
    wvt[:hd, :WINDOW] = wv[:WINDOW, :].astype(F32).T.astype(BF16)
    loads[5].wait()

    k2 = [remote(gath.at[0, core, :, z], gath.at[0, core, :, z], z2_sem, d, ctx=z_peer(d)) for d in range(1, nz)]
    v2 = [remote(gath.at[1, core, y], gath.at[1, core, y], y2_sem, d, ctx=y_peer(d)) for d in range(1, ny)]
    swap = remote(gath.at[:, core], gath.at[:, core], core_sem, 0, ctx=partner)

    def second():
        for c in k1 + v1:
            c.wait()
        for c in k2 + v2:
            c.start()

    def third():
        for c in k2 + v2:
            c.wait()
        swap.start()

    def head_cols(h):
        return pl.ds(pl.multiple_of(h * hd, hd), hd)

    def fold(s):
        return jnp.max(s.reshape(s.shape[0] // 8, 8, s.shape[1]), axis=0)

    def near_scores(h, s_ref, c_ref):
        for i in range(tok // HALF):
            cols = slice(i * HALF, (i + 1) * HALF)
            s = lax.dot_general(
                wk[i * HALF : i * HALF + width, :], q_v[cols, head_cols(h)], NT,
                preferred_element_type=F32,
            )
            s = s + near_bias[:, cols]
            s_ref[:, cols] = s
            c_ref[:, cols] = fold(s)

    def near_values(h, s_ref, c_ref):
        m = jnp.max(c_ref[...], axis=0, keepdims=True) * scale
        e = jnp.exp2(s_ref[...] * scale - m).astype(BF16)
        for i in range(tok // HALF):
            cols = slice(i * HALF, (i + 1) * HALF)
            o = jnp.dot(wvt[:, i * HALF : i * HALF + width], e[:, cols], preferred_element_type=F32)
            near_ref[h, :, cols] = o[:hd] * (1.0 / o[hd : hd + 1])

    near_scores(0, s0, c0)

    def near_group(j, carry):
        for u in range(0, UNROLL, 2):
            h = UNROLL * j + u
            near_scores(h + 1, s1, c1)
            near_values(h, s0, c0)
            near_scores(jnp.minimum(h + 2, heads - 2), s0, c0)
            near_values(h + 1, s1, c1)
        pl.when(j == STEP2)(second)
        return carry

    lax.fori_loop(0, heads // UNROLL, near_group, 0)

    third()
    logits = gate_send[group].astype(F32)
    for d in range(1, nkv):
        gate_copies[d - 1].wait()
        logits = logits + gate_recv[d].astype(F32)
    gates[...] = jax.nn.sigmoid(logits)


    half = cvt.shape[1] // nc
    keys_all = gath.reshape(2, nc, half, hd)

    def far_scores(par, first, w, h, s_ref, c_ref, masked):
        k = keys_all[0, par, pl.ds(first, w), :]
        s = lax.dot_general(k, q_v[:, head_cols(h)], NT, preferred_element_type=F32)
        if masked:
            s = s + far_bias[par, :w, :]
        s_ref[:w, :] = s
        c_ref[...] = fold(s)

    def far_values(par, first, w, h, s_ref, c_ref, last):
        m_old = m_ref[pl.ds(h, 1), :]
        m = jnp.maximum(jnp.max(c_ref[...], axis=0, keepdims=True) * scale, m_old)
        e = jnp.exp2(s_ref[:w, :] * scale - m).astype(BF16)
        vt = cvt[:, pl.ds(pl.multiple_of(par * half + first, KC), w)]
        o = jnp.dot(vt, e, preferred_element_type=F32)
        o = acc_ref[h] * jnp.exp2(m_old - m) + o
        if last:
            r = o[:hd] * (gates[pl.ds(h, 1), :] / o[hd : hd + 1]) + near_ref[h] * gates[pl.ds(heads + h, 1), :]
            out_v[:, head_cols(h)] = r.T.astype(BF16)
        else:
            acc_ref[h] = o
            m_ref[pl.ds(h, 1), :] = m

    def far_sweep(par, first, w, masked, last):
        far_scores(par, first, w, 0, s0, c0, masked)

        def group_of_heads(j, carry):
            for u in range(0, UNROLL, 2):
                h = UNROLL * j + u
                far_scores(par, first, w, h + 1, s1, c1, masked)
                far_values(par, first, w, h, s0, c0, last)
                far_scores(par, first, w, jnp.minimum(h + 2, heads - 2), s0, c0, masked)
                far_values(par, first, w, h + 1, s1, c1, last)
            return carry

        lax.fori_loop(0, heads // UNROLL, group_of_heads, 0)

    for turn in range(nc):
        par = core if turn == 0 else 1 - core
        if turn:
            swap.wait()
        for i in range(ny):
            vals = gath[1, par, i].reshape(nz * nb, hd)
            cvt[:hd, pl.ds(pl.multiple_of(par * half + i * nz * nb, nz * nb), nz * nb)] = vals.astype(F32).T.astype(BF16)

        def whole(i, carry):
            far_sweep(par, pl.multiple_of(i * KC, KC), KC, False, False)
            return carry

        lax.fori_loop(0, nfull, whole, 0)
        rest = lax.rem(slot, per) * nb // PIECE
        for n in range(KC // PIECE):
            @pl.when(rest == n)
            def _():
                far_sweep(par, pl.multiple_of(nfull * KC, KC), (n + 1) * PIECE, True, turn == nc - 1)


PIECE = 128
STEP2 = 0
UNROLL = 4


def on_device(dims, queries, keys, values, inputs, gate_weight, comp_one, comp_two):
    ny, nz, nc, nkv, heads = dims
    tok = queries.shape[0]
    hd = keys.shape[2]
    depth = inputs.shape[1]
    hid = comp_one.shape[3]
    gate_rows = gate_weight.shape[1] * gate_weight.shape[2]
    cols = ny * nz * nc * (tok // STRIDE)
    q = queries.reshape(tok, heads * hd)
    gate_w = gate_weight.transpose(1, 2, 0).reshape(gate_rows, depth)
    any_spec = pl.BlockSpec(memory_space=pl.ANY)
    vm = pltpu.VMEM
    dma = pltpu.SemaphoreType.DMA
    width = WINDOW + HALF
    out = pl.pallas_call(
        functools.partial(kernel, dims),
        out_shape=jax.ShapeDtypeStruct((tok, heads * hd), BF16),
        in_specs=[pl.BlockSpec(memory_space=pltpu.HBM)] * 7,
        out_specs=pl.BlockSpec(memory_space=pltpu.VMEM),
        scratch_shapes=[
            vm((tok, heads * hd), BF16),
            vm((tok, depth), BF16),
            vm((gate_rows, depth), BF16),
            vm((2, BLOCK * hd, hid), BF16),
            vm((2, hid, hd), BF16),
            vm((WINDOW + tok, hd), BF16),
            vm((WINDOW + tok, hd), BF16),
            vm((2, STRIDE, hd), BF16),
            vm((2, STRIDE + tok, hd), F32),
            vm((hd + 16, WINDOW + tok), BF16),
            vm((2, nc, ny, nz, tok // STRIDE, hd), BF16),
            vm((hd + 16, cols), BF16),
            vm((nkv, 2 * heads, tok), BF16),
            vm((nkv, 2 * heads, tok), BF16),
            vm((2 * heads, tok), F32),
            vm((width, tok), F32),
            vm((width, tok), F32),
            vm((8, tok), F32),
            vm((8, tok), F32),
            vm((heads, tok), F32),
            vm((heads, hd + 16, tok), F32),
            vm((heads, hd, tok), F32),
            vm((nc, KC, tok), F32),
            vm((width, tok), F32),
            dma((8,)),
            dma((2, 2)),
            dma((2, 2)),
            dma((2, nkv)),
            dma((2, ny)),
            dma((2, nz)),
            dma((2, nz)),
            dma((2, ny)),
            dma((2, 1)),
        ],
        compiler_params=pltpu.CompilerParams(
            collective_id=0, has_side_effects=True, vmem_limit_bytes=44 * 1024 * 1024
        ),
        name="attend",
    )(*[pltpu.with_memory_space_constraint(a, pltpu.HBM) for a in (
        q,
        keys.reshape(tok, hd),
        values.reshape(tok, hd),
        inputs,
        gate_w,
        comp_one.reshape(comp_one.shape[1:]),
        comp_two.reshape(comp_two.shape[1:]),
    )])
    return out.reshape(tok, 1, heads * hd)


def solution(mesh):
    placed = (
        P("ctx", "kv", None),
        P("ctx", "kv", None),
        P("ctx", "kv", None),
        P("ctx", "kv"),
        P("kv", None, None),
        P("kv", None, None, None),
        P("kv", None, None, None),
    )
    dims = (4, mesh.shape["ctx"] // 8, 2, mesh.shape["kv"], 16)
    return jax.shard_map(
        functools.partial(on_device, dims),
        mesh=mesh, in_specs=placed, out_specs=P("ctx", "kv", None), check_vma=False,
    )
```

```python
import functools

import jax
import jax.numpy as jnp
from jax import lax
from jax.experimental import pallas as pl
from jax.experimental.pallas import tpu as pltpu
from jax.sharding import PartitionSpec as P

MESH = pl.DeviceIdType.MESH
F32 = jnp.float32
BF16 = jnp.bfloat16
BLOCK = 32
STRIDE = 16
WINDOW = 512
NEG = -1e30
LOG2E = 1.4426950408889634
NT = (((1,), (1,)), ((), ()))
KC = 512
HALF = 256


def kernel(
    dims,
    q_hbm, keys_hbm, values_hbm, inputs_hbm, gate_w_hbm, one_hbm, two_hbm,
    out_v,
    q_v, inp_v, gw_v, one_v, two_v,
    wk, wv, rim, kv_f32, wvt, gath, cvt, gate_send, gate_recv, gates,
    s0, s1, c0, c1, m_ref, acc_ref, near_ref, far_bias, near_bias,
    in_sem, rim_sem, win_sem, gate_sem, y1_sem, z1_sem, z2_sem, y2_sem, core_sem,
):
    ny, nz, nc, nkv, heads = dims
    n_ctx = ny * nz * nc
    me = lax.axis_index("ctx")
    group = lax.axis_index("kv")
    y, z, core = me // (nz * nc), (me // nc) % nz, me % nc
    tok = q_v.shape[0]
    hd = wk.shape[1]
    scale = hd ** -0.5 * LOG2E
    right, left = lax.rem(me + 1, n_ctx), lax.rem(me + n_ctx - 1, n_ctx)

    def ctx_of(yy, zz, cc):
        return (yy * nz + zz) * nc + cc

    y_peer = lambda d: ctx_of(lax.rem(y + d, ny), z, core)
    z_peer = lambda d: ctx_of(y, lax.rem(z + d, nz), core)
    partner = ctx_of(y, z, 1 - core)
    kv_peer = lambda d: lax.rem(group + d, nkv)

    def load(src, dst, n):
        return pltpu.make_async_copy(src, dst, in_sem.at[n])

    loads = [
        load(keys_hbm, wk.at[pl.ds(WINDOW, tok), :], 0),
        load(values_hbm, wv.at[pl.ds(WINDOW, tok), :], 1),
        load(one_hbm.at[0], one_v.at[0], 2),
        load(one_hbm.at[1], one_v.at[1], 3),
        load(two_hbm, two_v, 4),
        load(q_hbm, q_v, 7),
        load(inputs_hbm, inp_v, 5),
        load(gate_w_hbm, gw_v, 6),
    ]
    for c in loads[:5]:
        c.start()

    barrier = pltpu.get_barrier_semaphore()
    n_sig = 0
    for d in range(1, ny):
        pl.semaphore_signal(barrier, inc=1, device_id={"ctx": y_peer(d)}, device_id_type=MESH)
        n_sig += 1
    for d in range(1, nz):
        pl.semaphore_signal(barrier, inc=1, device_id={"ctx": z_peer(d)}, device_id_type=MESH)
        n_sig += 1
    for other in (partner, left, right):
        pl.semaphore_signal(barrier, inc=1, device_id={"ctx": other}, device_id_type=MESH)
        n_sig += 1
    for d in range(1, nkv):
        pl.semaphore_signal(barrier, inc=1, device_id={"kv": kv_peer(d)}, device_id_type=MESH)
        n_sig += 1

    loads[0].wait()
    loads[1].wait()
    kv_f32[0, pl.ds(STRIDE, tok), :] = wk[pl.ds(WINDOW, tok), :].astype(F32)
    kv_f32[1, pl.ds(STRIDE, tok), :] = wv[pl.ds(WINDOW, tok), :].astype(F32)

    pl.semaphore_wait(barrier, n_sig)

    def remote(src, dst, sems, n, **where):
        return pltpu.make_async_remote_copy(
            src_ref=src, dst_ref=dst, send_sem=sems.at[0, n], recv_sem=sems.at[1, n],
            device_id=where, device_id_type=MESH,
        )

    tail = pl.ds(WINDOW + tok - STRIDE, STRIDE)
    rim_k = remote(wk.at[tail, :], rim.at[0], rim_sem, 0, ctx=right)
    rim_v = remote(wv.at[tail, :], rim.at[1], rim_sem, 1, ctx=right)
    rim_k.start()
    rim_v.start()
    win_k = remote(wk.at[pl.ds(tok, WINDOW), :], wk.at[pl.ds(0, WINDOW), :], win_sem, 0, ctx=right)
    win_v = remote(wv.at[pl.ds(tok, WINDOW), :], wv.at[pl.ds(0, WINDOW), :], win_sem, 1, ctx=right)
    win_k.start()
    win_v.start()

    rim_k.wait()
    rim_v.wait()
    kv_f32[0, :STRIDE, :] = rim[0].astype(F32)
    kv_f32[1, :STRIDE, :] = rim[1].astype(F32)
    loads[4].wait()
    nb = tok // STRIDE
    row = lax.broadcasted_iota(jnp.int32, (nb, hd), 0)
    loads[2].wait()
    loads[3].wait()
    for c in loads[5:]:
        c.start()

    def squeeze(s, carry):
        flat = jnp.concatenate(
            [kv_f32[s, pl.ds(b, nb, stride=STRIDE), :] for b in range(BLOCK)], axis=1
        ).astype(BF16)
        hidden = jnp.dot(flat, one_v[s], preferred_element_type=F32)
        hidden = jax.nn.gelu(hidden).astype(BF16)
        packed = jnp.dot(hidden, two_v[s], preferred_element_type=F32)
        packed = jnp.where((row == 0) & (me == 0), 0.0, packed)
        gath[s, core, y, z] = packed.astype(BF16)
        return carry

    lax.fori_loop(0, 2, squeeze, 0)
    k1 = [remote(gath.at[0, core, y, z], gath.at[0, core, y, z], y1_sem, d, ctx=y_peer(d)) for d in range(1, ny)]
    v1 = [remote(gath.at[1, core, y, z], gath.at[1, core, y, z], z1_sem, d, ctx=z_peer(d)) for d in range(1, nz)]
    for c in k1 + v1:
        c.start()

    slot = y * nz + z
    per = KC // nb
    nfull = slot // per
    for par in range(nc):
        i = lax.broadcasted_iota(jnp.int32, (KC, tok), 0) + nfull * KC
        ids = (i // nb) * (nc * nb) + par * nb + lax.rem(i, nb)
        at = lax.broadcasted_iota(jnp.int32, (KC, tok), 1) + tok * me
        far_bias[par] = jnp.where((ids * STRIDE + STRIDE - 1 <= at) | (ids == 0), 0.0, NEG)
    width = WINDOW + HALF
    for i in range(tok // HALF):
        w = lax.broadcasted_iota(jnp.int32, (width, HALF), 0)
        t = lax.broadcasted_iota(jnp.int32, (width, HALF), 1)
        low = jnp.where(me == 0, WINDOW - i * HALF, 0)
        near_bias[:, i * HALF : (i + 1) * HALF] = jnp.where(
            (w > t) & (w <= t + WINDOW) & (w >= low), 0.0, NEG
        )
    extra = wvt.shape[0] - hd
    one_row = lambda n: jnp.where(
        lax.broadcasted_iota(jnp.int32, (extra, n), 0) == 0, 1.0, 0.0
    ).astype(BF16)
    wvt[hd:, :] = one_row(WINDOW + tok)
    cvt[hd:, :] = one_row(cvt.shape[1])
    wvt[:hd, WINDOW:] = kv_f32[1, pl.ds(STRIDE, tok), :].T.astype(BF16)

    loads[6].wait()
    loads[7].wait()
    part = lax.dot_general(gw_v[...], inp_v[...], NT, preferred_element_type=F32)
    gate_send[...] = part.astype(BF16).reshape(gate_send.shape)
    gate_copies = []
    for d in range(1, nkv):
        to = kv_peer(d)
        gate_copies.append(remote(gate_send.at[to], gate_recv.at[d], gate_sem, d, kv=to))
        gate_copies[-1].start()

    win_k.wait()
    win_v.wait()
    wvt[:hd, :WINDOW] = wv[:WINDOW, :].astype(F32).T.astype(BF16)
    loads[5].wait()

    k2 = [remote(gath.at[0, core, :, z], gath.at[0, core, :, z], z2_sem, d, ctx=z_peer(d)) for d in range(1, nz)]
    v2 = [remote(gath.at[1, core, y], gath.at[1, core, y], y2_sem, d, ctx=y_peer(d)) for d in range(1, ny)]
    swap = remote(gath.at[:, core], gath.at[:, core], core_sem, 0, ctx=partner)

    def second():
        for c in k1 + v1:
            c.wait()
        for c in k2 + v2:
            c.start()

    def third():
        for c in k2 + v2:
            c.wait()
        swap.start()

    def head_cols(h):
        return pl.ds(pl.multiple_of(h * hd, hd), hd)

    def fold(s):
        return jnp.max(s.reshape(s.shape[0] // 8, 8, s.shape[1]), axis=0)

    def near_scores(h, s_ref, c_ref):
        for i in range(tok // HALF):
            cols = slice(i * HALF, (i + 1) * HALF)
            s = lax.dot_general(
                wk[i * HALF : i * HALF + width, :], q_v[cols, head_cols(h)], NT,
                preferred_element_type=F32,
            )
            s = s + near_bias[:, cols]
            s_ref[:width, cols] = s
            c_ref[:, cols] = fold(s)

    def near_values(h, s_ref, c_ref):
        m = jnp.max(c_ref[...], axis=0, keepdims=True) * scale
        e = jnp.exp2(s_ref[:width, :] * scale - m).astype(BF16)
        for i in range(tok // HALF):
            cols = slice(i * HALF, (i + 1) * HALF)
            o = jnp.dot(wvt[:, i * HALF : i * HALF + width], e[:, cols], preferred_element_type=F32)
            near_ref[h, :, cols] = o[:hd] * (1.0 / o[hd : hd + 1])

    near_scores(0, s0, c0)

    def near_group(j, carry):
        for u in range(0, UNROLL, 2):
            h = UNROLL * j + u
            near_scores(h + 1, s1, c1)
            near_values(h, s0, c0)
            near_scores(jnp.minimum(h + 2, heads - 2), s0, c0)
            near_values(h + 1, s1, c1)
        pl.when(j == STEP2)(second)
        return carry

    lax.fori_loop(0, heads // UNROLL, near_group, 0)

    third()
    logits = gate_send[group].astype(F32)
    for d in range(1, nkv):
        gate_copies[d - 1].wait()
        logits = logits + gate_recv[d].astype(F32)
    gates[...] = jax.nn.sigmoid(logits)


    half = cvt.shape[1] // nc
    keys_all = gath.reshape(2, nc, half, hd)

    def far_scores(par, w, h, s_ref, c_ref):
        k = keys_all[0, par, :w, :]
        s = lax.dot_general(k, q_v[:, head_cols(h)], NT, preferred_element_type=F32)
        free = (w - 1) // KC * KC
        end = s[free:] + far_bias[par, : w - free, :]
        top = fold(end)
        if free:
            s_ref[:free, :] = s[:free]
            top = jnp.maximum(top, fold(s[:free]))
        s_ref[free:w, :] = end
        c_ref[...] = top

    def far_values(par, w, h, s_ref, c_ref, last):
        m = jnp.maximum(jnp.max(c_ref[...], axis=0, keepdims=True) * scale, 0.0)
        if last:
            m_old = m_ref[pl.ds(h, 1), :]
            m = jnp.maximum(m, m_old)
        e = jnp.exp2(s_ref[:w, :] * scale - m).astype(BF16)
        vt = cvt[:, pl.ds(pl.multiple_of(par * half, half), w)]
        o = jnp.dot(vt, e, preferred_element_type=F32)
        if last:
            o = acc_ref[h] * jnp.exp2(m_old - m) + o
            r = o[:hd] * (gates[pl.ds(h, 1), :] / o[hd : hd + 1]) + near_ref[h] * gates[pl.ds(heads + h, 1), :]
            out_v[:, head_cols(h)] = r.T.astype(BF16)
        else:
            acc_ref[h] = o
            m_ref[pl.ds(h, 1), :] = m

    def far_sweep(par, w, last):
        unroll = UNROLL if w <= KC else WIDE
        far_scores(par, w, 0, s0, c0)

        def group_of_heads(j, carry):
            for u in range(0, unroll, 2):
                h = unroll * j + u
                far_scores(par, w, h + 1, s1, c1)
                far_values(par, w, h, s0, c0, last)
                far_scores(par, w, jnp.minimum(h + 2, heads - 2), s0, c0)
                far_values(par, w, h + 1, s1, c1, last)
            return carry

        lax.fori_loop(0, heads // unroll, group_of_heads, 0)

    for turn in range(nc):
        par = core if turn == 0 else 1 - core
        if turn:
            swap.wait()
        for i in range(ny):
            vals = gath[1, par, i].reshape(nz * nb, hd)
            cvt[:hd, pl.ds(pl.multiple_of(par * half + i * nz * nb, nz * nb), nz * nb)] = vals.astype(F32).T.astype(BF16)

        need = (slot + 1) * nb
        lower = 0
        for w in WIDTHS:
            @pl.when((need > lower) & (need <= w))
            def _():
                far_sweep(par, w, turn == nc - 1)

            lower = w


WIDTHS = (512, 768, 896, 1024)
WIDE = 4
STEP2 = 0
UNROLL = 4


def on_device(dims, queries, keys, values, inputs, gate_weight, comp_one, comp_two):
    ny, nz, nc, nkv, heads = dims
    tok = queries.shape[0]
    hd = keys.shape[2]
    depth = inputs.shape[1]
    hid = comp_one.shape[3]
    gate_rows = gate_weight.shape[1] * gate_weight.shape[2]
    cols = ny * nz * nc * (tok // STRIDE)
    q = queries.reshape(tok, heads * hd)
    gate_w = gate_weight.transpose(1, 2, 0).reshape(gate_rows, depth)
    any_spec = pl.BlockSpec(memory_space=pl.ANY)
    vm = pltpu.VMEM
    dma = pltpu.SemaphoreType.DMA
    width = WINDOW + HALF
    out = pl.pallas_call(
        functools.partial(kernel, dims),
        out_shape=jax.ShapeDtypeStruct((tok, heads * hd), BF16),
        in_specs=[pl.BlockSpec(memory_space=pltpu.HBM)] * 7,
        out_specs=pl.BlockSpec(memory_space=pltpu.VMEM),
        scratch_shapes=[
            vm((tok, heads * hd), BF16),
            vm((tok, depth), BF16),
            vm((gate_rows, depth), BF16),
            vm((2, BLOCK * hd, hid), BF16),
            vm((2, hid, hd), BF16),
            vm((WINDOW + tok, hd), BF16),
            vm((WINDOW + tok, hd), BF16),
            vm((2, STRIDE, hd), BF16),
            vm((2, STRIDE + tok, hd), F32),
            vm((hd + 16, WINDOW + tok), BF16),
            vm((2, nc, ny, nz, tok // STRIDE, hd), BF16),
            vm((hd + 16, cols), BF16),
            vm((nkv, 2 * heads, tok), BF16),
            vm((nkv, 2 * heads, tok), BF16),
            vm((2 * heads, tok), F32),
            vm((cols // nc, tok), F32),
            vm((cols // nc, tok), F32),
            vm((8, tok), F32),
            vm((8, tok), F32),
            vm((heads, tok), F32),
            vm((heads, hd + 16, tok), F32),
            vm((heads, hd, tok), F32),
            vm((nc, KC, tok), F32),
            vm((width, tok), F32),
            dma((8,)),
            dma((2, 2)),
            dma((2, 2)),
            dma((2, nkv)),
            dma((2, ny)),
            dma((2, nz)),
            dma((2, nz)),
            dma((2, ny)),
            dma((2, 1)),
        ],
        compiler_params=pltpu.CompilerParams(
            collective_id=0, has_side_effects=True, vmem_limit_bytes=44 * 1024 * 1024
        ),
        name="attend",
    )(*[pltpu.with_memory_space_constraint(a, pltpu.HBM) for a in (
        q,
        keys.reshape(tok, hd),
        values.reshape(tok, hd),
        inputs,
        gate_w,
        comp_one.reshape(comp_one.shape[1:]),
        comp_two.reshape(comp_two.shape[1:]),
    )])
    return out.reshape(tok, 1, heads * hd)


def solution(mesh):
    placed = (
        P("ctx", "kv", None),
        P("ctx", "kv", None),
        P("ctx", "kv", None),
        P("ctx", "kv"),
        P("kv", None, None),
        P("kv", None, None, None),
        P("kv", None, None, None),
    )
    dims = (4, mesh.shape["ctx"] // 8, 2, mesh.shape["kv"], 16)
    return jax.shard_map(
        functools.partial(on_device, dims),
        mesh=mesh, in_specs=placed, out_specs=P("ctx", "kv", None), check_vma=False,
    )
```

```python
import functools

import jax
import jax.numpy as jnp
from jax import lax
from jax.experimental import pallas as pl
from jax.experimental.pallas import tpu as pltpu
from jax.sharding import PartitionSpec as P

MESH = pl.DeviceIdType.MESH
F32 = jnp.float32
BF16 = jnp.bfloat16
BLOCK = 32
STRIDE = 16
WINDOW = 512
NEG = -1e30
LOG2E = 1.4426950408889634
NT = (((1,), (1,)), ((), ()))
KC = 512
HALF = 256


def kernel(
    dims,
    q_hbm, keys_hbm, values_hbm, inputs_hbm, gate_w_hbm, one_hbm, two_hbm,
    out_v,
    q_v, inp_v, gw_v, one_v, two_v,
    wk, wv, rim, kv_f32, wvt, gath, cvt, gate_send, gate_recv, gates,
    s0, s1, c0, c1, m_ref, acc_ref, near_ref, far_bias, near_bias,
    in_sem, rim_sem, win_sem, gate_sem, y1_sem, z1_sem, z2_sem, y2_sem, core_sem,
):
    ny, nz, nc, nkv, heads = dims
    n_ctx = ny * nz * nc
    me = lax.axis_index("ctx")
    group = lax.axis_index("kv")
    y, z, core = me // (nz * nc), (me // nc) % nz, me % nc
    tok = q_v.shape[0]
    hd = wk.shape[1]
    scale = hd ** -0.5 * LOG2E
    right, left = lax.rem(me + 1, n_ctx), lax.rem(me + n_ctx - 1, n_ctx)

    def ctx_of(yy, zz, cc):
        return (yy * nz + zz) * nc + cc

    y_peer = lambda d: ctx_of(lax.rem(y + d, ny), z, core)
    z_peer = lambda d: ctx_of(y, lax.rem(z + d, nz), core)
    partner = ctx_of(y, z, 1 - core)
    kv_peer = lambda d: lax.rem(group + d, nkv)

    def load(src, dst, n):
        return pltpu.make_async_copy(src, dst, in_sem.at[n])

    loads = [
        load(keys_hbm, wk.at[pl.ds(WINDOW, tok), :], 0),
        load(values_hbm, wv.at[pl.ds(WINDOW, tok), :], 1),
        load(one_hbm.at[0], one_v.at[0], 2),
        load(one_hbm.at[1], one_v.at[1], 3),
        load(two_hbm, two_v, 4),
        load(q_hbm, q_v, 7),
        load(inputs_hbm, inp_v, 5),
        load(gate_w_hbm, gw_v, 6),
    ]
    for c in loads[:5]:
        c.start()

    barrier = pltpu.get_barrier_semaphore()
    n_sig = 0
    for d in range(1, ny):
        pl.semaphore_signal(barrier, inc=1, device_id={"ctx": y_peer(d)}, device_id_type=MESH)
        n_sig += 1
    for d in range(1, nz):
        pl.semaphore_signal(barrier, inc=1, device_id={"ctx": z_peer(d)}, device_id_type=MESH)
        n_sig += 1
    for other in (partner, left, right):
        pl.semaphore_signal(barrier, inc=1, device_id={"ctx": other}, device_id_type=MESH)
        n_sig += 1
    for d in range(1, nkv):
        pl.semaphore_signal(barrier, inc=1, device_id={"kv": kv_peer(d)}, device_id_type=MESH)
        n_sig += 1

    loads[0].wait()
    loads[1].wait()
    kv_f32[0, pl.ds(STRIDE, tok), :] = wk[pl.ds(WINDOW, tok), :].astype(F32)
    kv_f32[1, pl.ds(STRIDE, tok), :] = wv[pl.ds(WINDOW, tok), :].astype(F32)

    pl.semaphore_wait(barrier, n_sig)

    def remote(src, dst, sems, n, **where):
        return pltpu.make_async_remote_copy(
            src_ref=src, dst_ref=dst, send_sem=sems.at[0, n], recv_sem=sems.at[1, n],
            device_id=where, device_id_type=MESH,
        )

    tail = pl.ds(WINDOW + tok - STRIDE, STRIDE)
    rim_k = remote(wk.at[tail, :], rim.at[0], rim_sem, 0, ctx=right)
    rim_v = remote(wv.at[tail, :], rim.at[1], rim_sem, 1, ctx=right)
    rim_k.start()
    rim_v.start()
    win_k = remote(wk.at[pl.ds(tok, WINDOW), :], wk.at[pl.ds(0, WINDOW), :], win_sem, 0, ctx=right)
    win_v = remote(wv.at[pl.ds(tok, WINDOW), :], wv.at[pl.ds(0, WINDOW), :], win_sem, 1, ctx=right)
    win_k.start()
    win_v.start()

    rim_k.wait()
    rim_v.wait()
    kv_f32[0, :STRIDE, :] = rim[0].astype(F32)
    kv_f32[1, :STRIDE, :] = rim[1].astype(F32)
    loads[4].wait()
    nb = tok // STRIDE
    row = lax.broadcasted_iota(jnp.int32, (nb, hd), 0)
    loads[2].wait()
    loads[3].wait()
    for c in loads[5:]:
        c.start()

    def squeeze(s, carry):
        flat = jnp.concatenate(
            [kv_f32[s, pl.ds(b, nb, stride=STRIDE), :] for b in range(BLOCK)], axis=1
        ).astype(BF16)
        hidden = jnp.dot(flat, one_v[s], preferred_element_type=F32)
        hidden = jax.nn.gelu(hidden).astype(BF16)
        packed = jnp.dot(hidden, two_v[s], preferred_element_type=F32)
        packed = jnp.where((row == 0) & (me == 0), 0.0, packed)
        gath[s, core, y, z] = packed.astype(BF16)
        return carry

    lax.fori_loop(0, 2, squeeze, 0)
    k1 = [remote(gath.at[0, core, y, z], gath.at[0, core, y, z], y1_sem, d, ctx=y_peer(d)) for d in range(1, ny)]
    v1 = [remote(gath.at[1, core, y, z], gath.at[1, core, y, z], z1_sem, d, ctx=z_peer(d)) for d in range(1, nz)]
    for c in k1 + v1:
        c.start()

    slot = y * nz + z
    per = KC // nb
    nfull = slot // per
    for par in range(nc):
        i = lax.broadcasted_iota(jnp.int32, (KC, tok), 0) + nfull * KC
        ids = (i // nb) * (nc * nb) + par * nb + lax.rem(i, nb)
        at = lax.broadcasted_iota(jnp.int32, (KC, tok), 1) + tok * me
        far_bias[par] = jnp.where((ids * STRIDE + STRIDE - 1 <= at) | (ids == 0), 0.0, NEG)
    width = WINDOW + HALF
    for i in range(tok // HALF):
        w = lax.broadcasted_iota(jnp.int32, (width, HALF), 0)
        t = lax.broadcasted_iota(jnp.int32, (width, HALF), 1)
        low = jnp.where(me == 0, WINDOW - i * HALF, 0)
        near_bias[:, i * HALF : (i + 1) * HALF] = jnp.where(
            (w > t) & (w <= t + WINDOW) & (w >= low), 0.0, NEG
        )
    extra = wvt.shape[0] - hd
    one_row = lambda n: jnp.where(
        lax.broadcasted_iota(jnp.int32, (extra, n), 0) == 0, 1.0, 0.0
    ).astype(BF16)
    wvt[hd:, :] = one_row(WINDOW + tok)
    cvt[hd:, :] = one_row(cvt.shape[1])
    wvt[:hd, WINDOW:] = kv_f32[1, pl.ds(STRIDE, tok), :].T.astype(BF16)

    loads[6].wait()
    loads[7].wait()
    part = lax.dot_general(gw_v[...], inp_v[...], NT, preferred_element_type=F32)
    gate_send[...] = part.astype(BF16).reshape(gate_send.shape)
    gate_copies = []
    for d in range(1, nkv):
        to = kv_peer(d)
        gate_copies.append(remote(gate_send.at[to], gate_recv.at[d], gate_sem, d, kv=to))
        gate_copies[-1].start()

    win_k.wait()
    win_v.wait()
    wvt[:hd, :WINDOW] = wv[:WINDOW, :].astype(F32).T.astype(BF16)
    loads[5].wait()

    k2 = [remote(gath.at[0, core, :, z], gath.at[0, core, :, z], z2_sem, d, ctx=z_peer(d)) for d in range(1, nz)]
    v2 = [remote(gath.at[1, core, y], gath.at[1, core, y], y2_sem, d, ctx=y_peer(d)) for d in range(1, ny)]
    swap = remote(gath.at[:, core], gath.at[:, core], core_sem, 0, ctx=partner)

    def second():
        for c in k1 + v1:
            c.wait()
        for c in k2 + v2:
            c.start()

    def third():
        for c in k2 + v2:
            c.wait()
        swap.start()

    def head_cols(h):
        return pl.ds(pl.multiple_of(h * hd, hd), hd)

    def fold(s):
        return jnp.max(s.reshape(s.shape[0] // 8, 8, s.shape[1]), axis=0)

    def near_scores(h, s_ref, c_ref):
        for i in range(tok // HALF):
            cols = slice(i * HALF, (i + 1) * HALF)
            s = lax.dot_general(
                wk[i * HALF : i * HALF + width, :], q_v[cols, head_cols(h)], NT,
                preferred_element_type=F32,
            )
            s = s + near_bias[:, cols]
            s_ref[:width, cols] = s
            c_ref[:, cols] = fold(s)

    def near_values(h, s_ref, c_ref):
        m = jnp.max(c_ref[...], axis=0, keepdims=True) * scale
        e = jnp.exp2(s_ref[:width, :] * scale - m).astype(BF16)
        for i in range(tok // HALF):
            cols = slice(i * HALF, (i + 1) * HALF)
            o = jnp.dot(wvt[:, i * HALF : i * HALF + width], e[:, cols], preferred_element_type=F32)
            near_ref[h, :, cols] = o[:hd] * (1.0 / o[hd : hd + 1])

    near_scores(0, s0, c0)

    def near_group(j, carry):
        for u in range(0, UNROLL, 2):
            h = UNROLL * j + u
            near_scores(h + 1, s1, c1)
            near_values(h, s0, c0)
            near_scores(jnp.minimum(h + 2, heads - 2), s0, c0)
            near_values(h + 1, s1, c1)
        pl.when(j == STEP2)(second)
        return carry

    lax.fori_loop(0, heads // UNROLL, near_group, 0)

    third()
    half = cvt.shape[1] // nc
    keys_all = gath.reshape(2, nc, half, hd)

    def far_scores(par, w, h, s_ref, c_ref):
        k = keys_all[0, par, :w, :]
        s = lax.dot_general(k, q_v[:, head_cols(h)], NT, preferred_element_type=F32)
        free = (w - 1) // KC * KC
        end = s[free:] + far_bias[par, : w - free, :]
        top = fold(end)
        if free:
            s_ref[:free, :] = s[:free]
            top = jnp.maximum(top, fold(s[:free]))
        s_ref[free:w, :] = end
        c_ref[...] = top

    def far_values(par, w, h, s_ref, c_ref, last):
        m = jnp.maximum(jnp.max(c_ref[...], axis=0, keepdims=True) * scale, 0.0)
        if last:
            m_old = m_ref[pl.ds(h, 1), :]
            m = jnp.maximum(m, m_old)
        e = jnp.exp2(s_ref[:w, :] * scale - m).astype(BF16)
        vt = cvt[:, pl.ds(pl.multiple_of(par * half, half), w)]
        o = jnp.dot(vt, e, preferred_element_type=F32)
        if last:
            o = acc_ref[h] * jnp.exp2(m_old - m) + o
            r = o[:hd] * (gates[pl.ds(h, 1), :] / o[hd : hd + 1]) + near_ref[h] * gates[pl.ds(heads + h, 1), :]
            out_v[:, head_cols(h)] = r.T.astype(BF16)
        else:
            acc_ref[h] = o
            m_ref[pl.ds(h, 1), :] = m

    def far_sweep(par, w, last):
        unroll = UNROLL if w <= KC else WIDE
        far_scores(par, w, 0, s0, c0)

        def group_of_heads(j, carry):
            for u in range(0, unroll, 2):
                h = unroll * j + u
                far_scores(par, w, h + 1, s1, c1)
                far_values(par, w, h, s0, c0, last)
                far_scores(par, w, jnp.minimum(h + 2, heads - 2), s0, c0)
                far_values(par, w, h + 1, s1, c1, last)
            return carry

        lax.fori_loop(0, heads // unroll, group_of_heads, 0)

    for turn in range(nc):
        par = core if turn == 0 else 1 - core
        if turn:
            swap.wait()
            logits = gate_send[group].astype(F32)
            for d in range(1, nkv):
                gate_copies[d - 1].wait()
                logits = logits + gate_recv[d].astype(F32)
            gates[...] = jax.nn.sigmoid(logits)
        for i in range(ny):
            vals = gath[1, par, i].reshape(nz * nb, hd)
            cvt[:hd, pl.ds(pl.multiple_of(par * half + i * nz * nb, nz * nb), nz * nb)] = vals.astype(F32).T.astype(BF16)

        need = (slot + 1) * nb
        lower = 0
        for w in WIDTHS:
            @pl.when((need > lower) & (need <= w))
            def _():
                far_sweep(par, w, turn == nc - 1)

            lower = w


WIDTHS = (512, 768, 896, 1024)
WIDE = 4
STEP2 = 0
UNROLL = 4


def on_device(dims, queries, keys, values, inputs, gate_weight, comp_one, comp_two):
    ny, nz, nc, nkv, heads = dims
    tok = queries.shape[0]
    hd = keys.shape[2]
    depth = inputs.shape[1]
    hid = comp_one.shape[3]
    gate_rows = gate_weight.shape[1] * gate_weight.shape[2]
    cols = ny * nz * nc * (tok // STRIDE)
    q = queries.reshape(tok, heads * hd)
    gate_w = gate_weight.transpose(1, 2, 0).reshape(gate_rows, depth)
    any_spec = pl.BlockSpec(memory_space=pl.ANY)
    vm = pltpu.VMEM
    dma = pltpu.SemaphoreType.DMA
    width = WINDOW + HALF
    out = pl.pallas_call(
        functools.partial(kernel, dims),
        out_shape=jax.ShapeDtypeStruct((tok, heads * hd), BF16),
        in_specs=[pl.BlockSpec(memory_space=pltpu.HBM)] * 7,
        out_specs=pl.BlockSpec(memory_space=pltpu.VMEM),
        scratch_shapes=[
            vm((tok, heads * hd), BF16),
            vm((tok, depth), BF16),
            vm((gate_rows, depth), BF16),
            vm((2, BLOCK * hd, hid), BF16),
            vm((2, hid, hd), BF16),
            vm((WINDOW + tok, hd), BF16),
            vm((WINDOW + tok, hd), BF16),
            vm((2, STRIDE, hd), BF16),
            vm((2, STRIDE + tok, hd), F32),
            vm((hd + 16, WINDOW + tok), BF16),
            vm((2, nc, ny, nz, tok // STRIDE, hd), BF16),
            vm((hd + 16, cols), BF16),
            vm((nkv, 2 * heads, tok), BF16),
            vm((nkv, 2 * heads, tok), BF16),
            vm((2 * heads, tok), F32),
            vm((cols // nc, tok), F32),
            vm((cols // nc, tok), F32),
            vm((8, tok), F32),
            vm((8, tok), F32),
            vm((heads, tok), F32),
            vm((heads, hd + 16, tok), F32),
            vm((heads, hd, tok), F32),
            vm((nc, KC, tok), F32),
            vm((width, tok), F32),
            dma((8,)),
            dma((2, 2)),
            dma((2, 2)),
            dma((2, nkv)),
            dma((2, ny)),
            dma((2, nz)),
            dma((2, nz)),
            dma((2, ny)),
            dma((2, 1)),
        ],
        compiler_params=pltpu.CompilerParams(
            collective_id=0, has_side_effects=True, vmem_limit_bytes=44 * 1024 * 1024
        ),
        name="attend",
    )(*[pltpu.with_memory_space_constraint(a, pltpu.HBM) for a in (
        q,
        keys.reshape(tok, hd),
        values.reshape(tok, hd),
        inputs,
        gate_w,
        comp_one.reshape(comp_one.shape[1:]),
        comp_two.reshape(comp_two.shape[1:]),
    )])
    return out.reshape(tok, 1, heads * hd)


def solution(mesh):
    placed = (
        P("ctx", "kv", None),
        P("ctx", "kv", None),
        P("ctx", "kv", None),
        P("ctx", "kv"),
        P("kv", None, None),
        P("kv", None, None, None),
        P("kv", None, None, None),
    )
    dims = (4, mesh.shape["ctx"] // 8, 2, mesh.shape["kv"], 16)
    return jax.shard_map(
        functools.partial(on_device, dims),
        mesh=mesh, in_specs=placed, out_specs=P("ctx", "kv", None), check_vma=False,
    )
```
